32 devices in a mesh: row: 2 (over core), col: 16 (over z, y, x).
Axes of the slice: x: 2, y: 2, z: 4, core: 2. Of those that a mesh axis runs over, the one named last changes fastest.
Arguments:
- edge: bfloat16 [1024, 4096], P('row', 'col'), may hold values from -6 to 6
- double_layer: bfloat16 [4096, 8192], P(None, 'col'), may hold values from -0.25 to 0.25
- projector: bfloat16 [1024, 2048], P('row'), may hold values from -0.25 to 0.25
- charge_in: int32 [32], replicated, may hold values from 0 to 7
- charge_out: int32 [64], P('col'), may hold values from 0 to 7
- allowed: int32 [8, 8], replicated, may hold values from 0 to 1, as said below
- owner_slot_tile: int32 [16], replicated, may hold values from 0 to 15, each once
Outputs:
- contracted: bfloat16 [1024, 8192], P('row', 'col')
- corner: bfloat16 [2048, 8192], P('row', 'col')
The draws below stay inside these ranges and needn't reach their ends.
Inputs may be any that keep to these rules, and one draw needn't show every extreme that they name: `owner_slot_tile`: each tile index appears once. Each charge has exactly one allowed partner charge, and every charge is the partner of exactly one charge.
All inputs are finite; a program needn't handle non-finite values.
Results may differ from the reference program's by a relative error of at most 0.005.
Values may be sent and summed in bfloat16 or wider, within the bound.
No kernel may reach another device: no remote copies, remote signals or barrier semaphores. Data moves between devices by JAX's collectives and lax.ppermute only.
A program may use at most 128 MiB of HBM per device.

```python
import jax
import jax.numpy as jnp
from jax import lax

TILE = 128
CHARGES = 8
M = 2048
R = 1024
K = 4096
N = 8192
KTILES = 32
NTILES = 64
CORNER_TILES = 16


def draw_allowed(key, part):
    shift = jax.random.randint(jax.random.fold_in(key, 17), (), 0, CHARGES)
    levels = jnp.arange(CHARGES, dtype=jnp.int32)
    partner_slot = (levels + shift) % CHARGES
    return (levels[None, :] == partner_slot[:, None]).astype(jnp.int32)


def touch_ends(values, key, low, high):
    place = [jax.random.randint(jax.random.fold_in(key, axis), (), 0, length) for axis, length in enumerate(values.shape)]
    main_axis = values.shape.index(max(values.shape))
    neighbour = place[:main_axis] + [(place[main_axis] + 1) % values.shape[main_axis]] + place[main_axis + 1:]
    return values.at[tuple(place)].set(low).at[tuple(neighbour)].set(high)


def spiked(array, key, source, target, parts, factor):
    owner, partner = [(jnp.arange(array.shape[dim]) // (array.shape[dim] // parts)).reshape([-1 if axis == dim else 1 for axis in range(array.ndim)]) for dim in (source, target)]
    chosen = jax.random.permutation(key, parts)[partner]
    strong = (owner == chosen) | (owner == (partner + parts // 2) % parts)
    return jnp.where(strong, factor * array, array)


def block_levels(own_key, shape, split, smallest, high):
    def one(axis_at, blocks):
        draws = jax.random.uniform(jax.random.fold_in(jax.random.fold_in(own_key, 6), axis_at), (blocks,), jnp.float32, smallest / len(split), high / len(split))
        return jnp.repeat(jnp.exp(draws), shape[axis_at] // blocks).reshape((-1,) + (1,) * (len(shape) - axis_at - 1))

    loudness = one(*split[0])
    for cut in split[1:]:
        loudness = loudness * one(*cut)
    return loudness


def normal_values(rng, shape, deviation, most, pieces=(), held_as=jnp.bfloat16):
    entries = jax.random.normal(rng, shape, jnp.float32) * deviation
    if len(pieces) > 0:
        entries = block_levels(rng, shape, pieces, -0.22, 0.18) * entries
    return jnp.clip(entries, min=-most, max=most).astype(held_as)


def gaussian_with(own_key, dims, deviation, most, pieces, heavy, kind=jnp.bfloat16):
    array = deviation * jax.random.normal(own_key, dims, jnp.float32)
    if pieces:
        array = array * block_levels(own_key, dims, pieces, -0.22, 0.18)
    return jnp.clip(spiked(array, jax.random.fold_in(own_key, 3), *heavy), -most, most).astype(kind)


def setup_inputs(seed: int = 0) -> dict:
    key_list = jax.random.split(jax.random.key(seed), 8)
    return {
        "edge": normal_values(key_list[0], (R, K), 1.0, 6.0, ((0, 2), (1, 16))),
        "double_layer": normal_values(key_list[1], (K, N), (K // 8) ** -0.5, 0.25, ((1, 16),)),
        "projector": gaussian_with(key_list[2], (R, M), R ** -0.5, 0.25, ((0, 2),), (0, 1, 2, 2.0)),
        "charge_in": touch_ends(jax.random.randint(key_list[3], (KTILES,), 0, CHARGES), jax.random.fold_in(key_list[3], 1), 0, CHARGES - 1).astype(jnp.int32),
        "charge_out": touch_ends(jax.random.randint(key_list[4], (NTILES,), 0, CHARGES), jax.random.fold_in(key_list[4], 1), 0, CHARGES - 1).astype(jnp.int32),
        "allowed": draw_allowed(jax.random.fold_in(key_list[7], 71), 0),
        "owner_slot_tile": jax.random.permutation(key_list[6], CORNER_TILES).astype(jnp.int32),
    }


def block_mask(charge_in, charge_out, allowed):
    levels = jnp.arange(allowed.shape[0], dtype=jnp.int32)
    onehot_in = (charge_in[:, None] == levels[None, :]).astype(jnp.float32)
    onehot_out = (charge_out[:, None] == levels[None, :]).astype(jnp.float32)
    linked = jnp.dot(onehot_in, allowed.astype(jnp.float32), precision=lax.Precision.HIGHEST)
    linked = jnp.dot(linked, onehot_out.T, precision=lax.Precision.HIGHEST)
    return linked.astype(jnp.bfloat16)


def layer_under_mask(double_layer, blocks):
    incoming_tiles, out_tiles = blocks.shape
    shaped = double_layer.reshape(incoming_tiles, TILE, out_tiles, TILE)
    return (shaped * blocks[:, None, :, None]).reshape(incoming_tiles * TILE, out_tiles * TILE)


def owner_columns(owner_slot_tile):
    within_bounds = jnp.arange(TILE, dtype=jnp.int32)
    return (owner_slot_tile.astype(jnp.int32)[:, None] * TILE + within_bounds[None, :]).reshape(-1)


def reference(edge, double_layer, projector, charge_in, charge_out, allowed, owner_slot_tile):
    blocks = block_mask(charge_in, charge_out, allowed)
    masked_values = layer_under_mask(double_layer, blocks)
    contracted = jnp.dot(edge, masked_values, preferred_element_type=jnp.float32).astype(jnp.bfloat16)
    ordered = jnp.take(projector, owner_columns(owner_slot_tile), axis=1)
    corner = lax.dot_general(ordered, contracted, (((0,), (0,)), ((), ())), preferred_element_type=jnp.float32)
    return contracted, corner.astype(jnp.bfloat16)
```

```python
import functools

import jax
import jax.numpy as jnp
from jax import lax
from jax.experimental import pallas as pl
from jax.experimental.pallas import tpu as pltpu
from jax.sharding import PartitionSpec as P

TILE = 128

VMEM = pl.BlockSpec(memory_space=pltpu.VMEM)
SMEM = pl.BlockSpec(memory_space=pltpu.SMEM)


def absorb_body(count, fresh, last, kb, cin, cout, allowed, layer, *refs):
    edges, out, masked = refs[:count], refs[-2], refs[-1]
    depth = edges[0].shape[1]
    rows = edges[0].shape[0]
    for j in range(count):
        block = kb[j]
        for k in range(depth // TILE):
            charge = cin[block * (depth // TILE) + k]
            for c in range(layer.shape[1] // TILE):
                keep = allowed[charge, cout[c]] != 0
                at = pl.ds(pl.multiple_of(block * depth + k * TILE, TILE), TILE)
                tile = layer[at, c * TILE:(c + 1) * TILE]
                masked[j * depth + k * TILE:j * depth + (k + 1) * TILE, c * TILE:(c + 1) * TILE] = jnp.where(
                    keep, tile, jnp.zeros_like(tile)
                )
    step = 128
    for r in range(0, rows, step):
        total = None if fresh else refs[count][r:r + step, :]
        for j in range(count):
            term = jnp.dot(
                edges[j][r:r + step, :],
                masked[j * depth:(j + 1) * depth, :],
                preferred_element_type=jnp.float32,
            )
            total = term if total is None else total + term
        out[r:r + step, :] = total.astype(out.dtype)


def absorb(numbers, tables, layer, blocks, total, last):
    count, (rows, depth), columns = len(blocks), blocks[0].shape, layer.shape[1]
    kind = jnp.bfloat16 if last else jnp.float32
    extra = () if total is None else (total,)
    return pl.pallas_call(
        functools.partial(absorb_body, count, total is None, last),
        out_shape=jax.ShapeDtypeStruct((rows, columns), kind),
        in_specs=[SMEM] * 4 + [VMEM] * (1 + count + len(extra)),
        out_specs=VMEM,
        scratch_shapes=[pltpu.VMEM((count * depth, columns), jnp.bfloat16)],
        cost_estimate=pl.CostEstimate(
            flops=2 * count * rows * depth * columns, bytes_accessed=4 * count * depth * (rows + columns), transcendentals=0
        ),
        name="absorb",
    )(jnp.stack(numbers), *tables, layer, *blocks, *extra)


def order_body(slots, projector, out):
    del slots
    out[...] = projector[...].T


def order(slots, projector):
    rows, tiles = projector.shape[0], slots.shape[0]
    return pl.pallas_call(
        order_body,
        grid_spec=pltpu.PrefetchScalarGridSpec(
            num_scalar_prefetch=1,
            grid=(tiles,),
            in_specs=[pl.BlockSpec((rows, TILE), lambda t, s: (0, s[t]))],
            out_specs=pl.BlockSpec((TILE, rows), lambda t, s: (t, 0)),
        ),
        out_shape=jax.ShapeDtypeStruct((tiles * TILE, rows), projector.dtype),
        cost_estimate=pl.CostEstimate(flops=0, bytes_accessed=4 * tiles * TILE * rows, transcendentals=0),
        name="order",
    )(slots, projector)


def corner_body(fresh, ordered, contracted, *refs):
    out = refs[-1]
    step = 256
    for r in range(0, ordered.shape[0], step):
        term = jnp.dot(ordered[r:r + step, :], contracted[...], preferred_element_type=jnp.float32)
        if not fresh:
            term = term + refs[0][r:r + step, :]
        out[r:r + step, :] = term.astype(out.dtype)


def corner_part(ordered, contracted, total, last):
    extra = () if total is None else (total,)
    rows, depth = ordered.shape
    columns = contracted.shape[1]
    return pl.pallas_call(
        functools.partial(corner_body, total is None),
        out_shape=jax.ShapeDtypeStruct((rows, columns), jnp.bfloat16 if last else jnp.float32),
        in_specs=[VMEM] * (2 + len(extra)),
        out_specs=VMEM,
        cost_estimate=pl.CostEstimate(
            flops=2 * rows * depth * columns, bytes_accessed=2 * depth * (rows + columns), transcendentals=0
        ),
        name="corner",
    )(ordered, contracted, *extra)


def local(groups, n, edge, double_layer, projector, charge_in, charge_out, allowed, owner_slot_tile):
    planes = n // 4
    row, col = lax.axis_index("row"), lax.axis_index("col")

    def plane_shift(value, by):
        return lax.ppermute(value, "col", [(c, (c // 4 + by) % planes * 4 + c % 4) for c in range(n)])

    def across(value, which):
        flip = lambda r: which if r % 2 == 0 else 3 - which
        pairs = [(r * n + c, r * n + (c ^ flip(r))) for r in range(groups) for c in range(n)]
        return lax.ppermute(value, ("row", "col"), pairs)

    first = 1 + row % 2
    second = 3 - first

    def number(slot, flip):
        return ((col // 4 - slot + planes) % planes * 4 + col % 4) ^ flip

    own, left = {0: edge}, {}
    up = planes // 2
    one, other = {}, {}
    for s in range(1, up + 1):
        own[s] = plane_shift(own[s - 1], 1)
        if s < planes - s:
            own[planes - s] = plane_shift(own[(planes - s + 1) % planes], -1)

    parts = {}
    for s in range(planes):
        mine = own[s]
        if s == 1 and planes > 1:
            a, d = plane_shift(parts[0][1], 1), plane_shift(parts[0][3], 1)
            b = across(mine, 2)
        else:
            a = across(mine, 1)
            b = across(mine, 2)
            d = across(a, 2)
        parts[s] = (mine, a, b, d)

    tables = (charge_in, charge_out, allowed)
    names = lambda s: [number(s, 0), number(s, first), number(s, second), number(s, 3)]
    slots = [s for s in range(planes) if s != up] + [up]
    total = None
    for s in slots[:-1]:
        total = absorb(names(s), tables, double_layer, parts[s], total, False)
    s = slots[-1]
    total = absorb(names(s)[:3], tables, double_layer, parts[s][:3], total, False)
    contracted = absorb(names(s)[3:], tables, double_layer, parts[s][3:], total, True)

    share = owner_slot_tile.shape[0] // groups
    wanted = (jnp.arange(groups)[:, None] + row) % groups * share + jnp.arange(share)[None, :]
    ordered = order(owner_slot_tile[wanted.reshape(-1)], projector)
    ordered = ordered.reshape(groups, share * TILE, projector.shape[0])
    theirs = [ordered[0]]
    for k in range(1, groups):
        theirs.append(lax.ppermute(ordered[k], "row", [(r, (r + k) % groups) for r in range(groups)]))
    corner = None
    for k in range(groups):
        held = contracted
        if k:
            held = lax.ppermute(contracted, "row", [(r, (r + k) % groups) for r in range(groups)])
        corner = corner_part(theirs[k], held, corner, k == groups - 1)
    return contracted, corner


def solution(mesh):
    return jax.shard_map(
        functools.partial(local, mesh.shape["row"], mesh.shape["col"]),
        mesh=mesh,
        in_specs=(P("row", "col"), P(None, "col"), P("row", None), P(), P("col"), P(), P()),
        out_specs=(P("row", "col"), P("row", "col")),
        check_vma=False,
    )
```

```python
import functools

import jax
import jax.numpy as jnp
from jax import lax
from jax.experimental import pallas as pl
from jax.experimental.pallas import tpu as pltpu
from jax.sharding import PartitionSpec as P

TILE = 128

VMEM = pl.BlockSpec(memory_space=pltpu.VMEM)
SMEM = pl.BlockSpec(memory_space=pltpu.SMEM)


def near(*arrays):
    return [pltpu.with_memory_space_constraint(a, pltpu.VMEM) for a in arrays]


def grant(mebibytes):
    return pltpu.CompilerParams(vmem_limit_bytes=mebibytes << 20)


def absorb_body(planes, names, fresh, cin, cout, allowed, layer, *refs):
    count = len(names)
    edges, out, masked = refs[:count], refs[-2], refs[-1]
    depth, tiles = edges[0].shape[1], edges[0].shape[1] // TILE
    row, col = lax.axis_index("row"), lax.axis_index("col")
    plane, spot = lax.div(col, 4), lax.rem(col, 4)
    first = 1 + lax.rem(row, 2)
    flips = {"own": 0, "first": first, "second": 3 - first, "both": 3}
    for j, (slot, which) in enumerate(names):
        block = lax.rem(plane + (planes - slot), planes) * 4 + (spot ^ flips[which])
        for k in range(tiles):
            charge = cin[block * tiles + k]
            at = pl.ds(pl.multiple_of(block * depth + k * TILE, TILE), TILE)
            for c in range(layer.shape[1] // TILE):
                keep = allowed[charge, cout[c]] != 0
                tile = layer[at, c * TILE:(c + 1) * TILE]
                masked[j * depth + k * TILE:j * depth + (k + 1) * TILE, c * TILE:(c + 1) * TILE] = jnp.where(
                    keep, tile, jnp.zeros_like(tile)
                )
    wide = jnp.concatenate([e[...] for e in edges], axis=1)
    total = jnp.dot(wide, masked[...], preferred_element_type=jnp.float32)
    if not fresh:
        total = total + refs[count][...]
    out[...] = total.astype(out.dtype)


def absorb(planes, names, tables, layer, blocks, total, last):
    count, (rows, depth), columns = len(blocks), blocks[0].shape, layer.shape[1]
    extra = () if total is None else (total,)
    if last:
        shape = jax.ShapeDtypeStruct((rows, columns), jnp.bfloat16)
    else:
        shape = pltpu.VMEM((rows, columns), jnp.float32)
    return pl.pallas_call(
        functools.partial(absorb_body, planes, names, total is None),
        out_shape=shape,
        in_specs=[SMEM] * 3 + [VMEM] * (1 + count + len(extra)),
        out_specs=VMEM,
        scratch_shapes=[pltpu.VMEM((count * depth, columns), jnp.bfloat16)],
        compiler_params=grant(8),
        cost_estimate=pl.CostEstimate(
            flops=2 * count * rows * depth * columns, bytes_accessed=4 * count * depth * columns, transcendentals=0
        ),
        name="absorb",
    )(*tables, *near(layer, *blocks, *extra))


def order_body(groups, slots, projector, *outs):
    share = slots.shape[0] // groups
    row = lax.axis_index("row")
    for k in range(groups):
        for t in range(share):
            tile = slots[lax.rem(row + k, groups) * share + t]
            at = pl.ds(pl.multiple_of(tile * TILE, TILE), TILE)
            outs[k][t * TILE:(t + 1) * TILE, :] = projector[:, at].T


def order(groups, slots, projector):
    rows, share = projector.shape[0], slots.shape[0] // groups
    return pl.pallas_call(
        functools.partial(order_body, groups),
        out_shape=[pltpu.VMEM((share * TILE, rows), projector.dtype)] * groups,
        in_specs=[SMEM, VMEM],
        out_specs=[VMEM] * groups,
        compiler_params=grant(8),
        cost_estimate=pl.CostEstimate(flops=0, bytes_accessed=4 * projector.size, transcendentals=0),
        name="order",
    )(slots, *near(projector))


def corner_body(fresh, ordered, contracted, *refs):
    out = refs[-1]
    total = jnp.dot(ordered[...], contracted[...], preferred_element_type=jnp.float32)
    if not fresh:
        total = total + refs[0][...]
    out[...] = total.astype(out.dtype)


def corner_part(ordered, contracted, total, last):
    extra = () if total is None else (total,)
    rows, depth = ordered.shape
    columns = contracted.shape[1]
    if last:
        shape = jax.ShapeDtypeStruct((rows, columns), jnp.bfloat16)
    else:
        shape = pltpu.VMEM((rows, columns), jnp.float32)
    return pl.pallas_call(
        functools.partial(corner_body, total is None),
        out_shape=shape,
        in_specs=[VMEM] * (2 + len(extra)),
        out_specs=VMEM,
        compiler_params=grant(8),
        cost_estimate=pl.CostEstimate(
            flops=2 * rows * depth * columns, bytes_accessed=2 * depth * (rows + columns), transcendentals=0
        ),
        name="corner",
    )(*near(ordered, contracted, *extra))


def local(groups, n, edge, double_layer, projector, charge_in, charge_out, allowed, owner_slot_tile):
    planes = n // 4

    def plane_shift(value, by):
        return lax.ppermute(value, "col", [(c, (c // 4 + by) % planes * 4 + c % 4) for c in range(n)])

    def across(value, which):
        flip = lambda r: which if r % 2 == 0 else 3 - which
        pairs = [(r * n + c, r * n + (c ^ flip(r))) for r in range(groups) for c in range(n)]
        return lax.ppermute(value, ("row", "col"), pairs)

    own = {0: edge}
    up = planes // 2
    for s in range(1, up + 1):
        own[s] = plane_shift(own[s - 1], 1)
        if s < planes - s:
            own[planes - s] = plane_shift(own[(planes - s + 1) % planes], -1)

    parts = {}
    for s in range(planes):
        mine = own[s]
        b = across(mine, 2)
        if s == 1:
            a, d = plane_shift(parts[0][1], 1), plane_shift(parts[0][3], 1)
        else:
            a = across(mine, 1)
            d = across(a, 2)
        parts[s] = (mine, a, b, d)

    tables = (charge_in, charge_out, allowed)
    names = lambda s: [(s, "own"), (s, "first"), (s, "second"), (s, "both")]
    slots = [s for s in range(planes) if s != up] + [up]
    total = None
    for s in slots[:-1]:
        total = absorb(planes, names(s), tables, double_layer, parts[s], total, False)
    s = slots[-1]
    total = absorb(planes, names(s)[:3], tables, double_layer, parts[s][:3], total, False)
    contracted = absorb(planes, names(s)[3:], tables, double_layer, parts[s][3:], total, True)

    theirs = list(order(groups, owner_slot_tile, projector))
    for k in range(1, groups):
        theirs[k] = lax.ppermute(theirs[k], "row", [(r, (r + k) % groups) for r in range(groups)])
    corner = None
    for k in range(groups):
        held = contracted
        if k:
            held = lax.ppermute(contracted, "row", [(r, (r + k) % groups) for r in range(groups)])
        corner = corner_part(theirs[k], held, corner, k == groups - 1)
    return contracted, corner


def solution(mesh):
    return jax.shard_map(
        functools.partial(local, mesh.shape["row"], mesh.shape["col"]),
        mesh=mesh,
        in_specs=(P("row", "col"), P(None, "col"), P("row", None), P(), P("col"), P(), P()),
        out_specs=(P("row", "col"), P("row", "col")),
        check_vma=False,
    )
```

```python
import functools

import jax
import jax.numpy as jnp
from jax import lax
from jax.experimental import pallas as pl
from jax.experimental.pallas import tpu as pltpu
from jax.sharding import PartitionSpec as P


TILE = 128

VMEM = pl.BlockSpec(memory_space=pltpu.VMEM)
SMEM = pl.BlockSpec(memory_space=pltpu.SMEM)
FAR = pl.BlockSpec(memory_space=pl.ANY)


def near(*arrays):
    return [pltpu.with_memory_space_constraint(a, pltpu.VMEM) for a in arrays]


def far(*arrays):
    return [pltpu.with_memory_space_constraint(a, pltpu.HBM) for a in arrays]


def grant(mebibytes):
    return pltpu.CompilerParams(vmem_limit_bytes=mebibytes << 20)


def mask_body(cin, cout, allowed, layer, out, met, sems):
    rows, columns = layer.shape
    tiles = columns // TILE
    for q in range(allowed.shape[0]):
        bits = jnp.int32(0)
        for c in range(tiles):
            bits = bits + jnp.where(allowed[q, cout[c]] != 0, 1 << c, 0)
        met[q] = bits

    def fetch(k):
        at = pl.ds(k * TILE, TILE)
        return pltpu.make_async_copy(layer.at[at, :], out.at[at, :], sems.at[k])

    for k in range(rows // TILE):
        pl.when(met[cin[k]] != 0)(lambda k=k: fetch(k).start())
    for k in range(rows // TILE):
        bits = met[cin[k]]

        @pl.when(bits == 0)
        def _():
            out[k * TILE:(k + 1) * TILE, :] = jnp.zeros((TILE, columns), out.dtype)

    for k in range(rows // TILE):
        bits = met[cin[k]]

        @pl.when(bits != 0)
        def _():
            fetch(k).wait()
            for c in range(tiles):

                @pl.when(lax.bitwise_and(bits, 1 << c) == 0)
                def _():
                    out[k * TILE:(k + 1) * TILE, c * TILE:(c + 1) * TILE] = jnp.zeros((TILE, TILE), out.dtype)


def mask(tables, layer):
    return pl.pallas_call(
        mask_body,
        out_shape=pltpu.VMEM(layer.shape, layer.dtype),
        in_specs=[SMEM] * 3 + [FAR],
        out_specs=VMEM,
        scratch_shapes=[
            pltpu.SMEM((tables[2].shape[0],), jnp.int32),
            pltpu.SemaphoreType.DMA((layer.shape[0] // TILE,)),
        ],
        compiler_params=grant(8),
        cost_estimate=pl.CostEstimate(flops=0, bytes_accessed=2 * layer.size, transcendentals=0),
        name="mask",
    )(*far(*tables, layer))


def absorb_body(planes, names, fresh, masked, *refs):
    count = len(names)
    edges, out = refs[:count], refs[-1]
    depth = edges[0].shape[1]
    row, col = lax.axis_index("row"), lax.axis_index("col")
    plane, spot = lax.div(col, 4), lax.rem(col, 4)
    first = 1 + lax.rem(row, 2)
    flips = {"own": 0, "first": first, "second": 3 - first, "both": 3}
    layers = []
    for slot, which in names:
        block = lax.rem(plane + (planes - slot), planes) * 4 + (spot ^ flips[which])
        layers.append(masked[pl.ds(pl.multiple_of(block * depth, depth), depth), :])
    wide = jnp.concatenate([e[...] for e in edges], axis=1)
    total = jnp.dot(wide, jnp.concatenate(layers, axis=0), preferred_element_type=jnp.float32)
    if not fresh:
        total = total + refs[count][...]
    out[...] = total.astype(out.dtype)


def absorb(planes, names, masked, blocks, total, last):
    count, (rows, depth), columns = len(blocks), blocks[0].shape, masked.shape[1]
    extra = () if total is None else (total,)
    return pl.pallas_call(
        functools.partial(absorb_body, planes, names, total is None),
        out_shape=pltpu.VMEM((rows, columns), jnp.bfloat16 if last else jnp.float32),
        in_specs=[VMEM] * (1 + count + len(extra)),
        out_specs=VMEM,
        compiler_params=grant(8),
        cost_estimate=pl.CostEstimate(
            flops=2 * count * rows * depth * columns, bytes_accessed=4 * count * depth * columns, transcendentals=0
        ),
        name="absorb",
    )(*near(masked, *blocks, *extra))


def order_body(groups, chunks, slots, projector, *refs):
    outs, held, sems = refs[:groups], refs[-2], refs[-1]
    share = slots.shape[0] // groups
    step = projector.shape[0] // chunks
    row = lax.axis_index("row")
    copies = []
    for i in range(chunks):
        at = pl.ds(i * step, step)
        copies.append(pltpu.make_async_copy(projector.at[at, :], held.at[at, :], sems.at[i]))
        copies[-1].start()
    for i in range(chunks):
        copies[i].wait()
        for k in range(groups):
            for t in range(share):
                tile = slots[lax.rem(row + k, groups) * share + t]
                at = pl.ds(pl.multiple_of(tile * TILE, TILE), TILE)
                outs[k][t * TILE:(t + 1) * TILE, i * step:(i + 1) * step] = held[i * step:(i + 1) * step, at].T


def order(groups, slots, projector):
    chunks = 4
    rows, share = projector.shape[0], slots.shape[0] // groups
    return pl.pallas_call(
        functools.partial(order_body, groups, chunks),
        out_shape=[pltpu.VMEM((share * TILE, rows), projector.dtype)] * groups,
        in_specs=[SMEM, FAR],
        out_specs=[VMEM] * groups,
        scratch_shapes=[pltpu.VMEM(projector.shape, projector.dtype), pltpu.SemaphoreType.DMA((chunks,))],
        compiler_params=grant(8),
        cost_estimate=pl.CostEstimate(flops=0, bytes_accessed=4 * projector.size, transcendentals=0),
        name="order",
    )(*far(slots, projector))


def own_corner_body(ordered, contracted, total, kept, sem):
    copy = pltpu.make_async_copy(contracted, kept, sem)
    copy.start()
    total[...] = jnp.dot(ordered[...], contracted[...], preferred_element_type=jnp.float32)
    copy.wait()


def own_corner(ordered, contracted):
    (rows, depth), columns = ordered.shape, contracted.shape[1]
    return pl.pallas_call(
        own_corner_body,
        out_shape=[
            pltpu.VMEM((rows, columns), jnp.float32),
            jax.ShapeDtypeStruct(contracted.shape, contracted.dtype),
        ],
        in_specs=[VMEM] * 2,
        out_specs=[VMEM, FAR],
        scratch_shapes=[pltpu.SemaphoreType.DMA],
        compiler_params=grant(8),
        cost_estimate=pl.CostEstimate(flops=2 * rows * depth * columns, bytes_accessed=contracted.size, transcendentals=0),
        name="own_corner",
    )(*near(ordered, contracted))


def corner_body(chunks, ordered, contracted, total, out, held, sems):
    step = ordered.shape[0] // chunks
    copies = []
    for i in range(chunks):
        at = pl.ds(i * step, step)
        term = jnp.dot(ordered[at, :], contracted[...], preferred_element_type=jnp.float32)
        held[at, :] = (total[at, :] + term).astype(held.dtype)
        copies.append(pltpu.make_async_copy(held.at[at, :], out.at[at, :], sems.at[i]))
        copies[-1].start()
    for copy in copies:
        copy.wait()


def corner_sum(ordered, contracted, total):
    chunks, kind = 4, jnp.bfloat16
    (rows, depth), columns = ordered.shape, contracted.shape[1]
    return pl.pallas_call(
        functools.partial(corner_body, chunks),
        out_shape=jax.ShapeDtypeStruct((rows, columns), kind),
        in_specs=[VMEM] * 3,
        out_specs=FAR,
        scratch_shapes=[pltpu.VMEM((rows, columns), kind), pltpu.SemaphoreType.DMA((chunks,))],
        compiler_params=grant(8),
        cost_estimate=pl.CostEstimate(flops=2 * rows * depth * columns, bytes_accessed=2 * rows * columns, transcendentals=0),
        name="corner",
    )(*near(ordered, contracted, total))


def more_corner_body(ordered, contracted, total, out):
    out[...] = total[...] + jnp.dot(ordered[...], contracted[...], preferred_element_type=jnp.float32)


def more_corner(ordered, contracted, total):
    return pl.pallas_call(
        more_corner_body,
        out_shape=pltpu.VMEM(total.shape, total.dtype),
        in_specs=[VMEM] * 3,
        out_specs=VMEM,
        compiler_params=grant(8),
        name="more_corner",
    )(*near(ordered, contracted, total))


def plan(planes):
    up = planes // 2
    four = ("own", "first", "second", "both")
    late = []
    for s in range(1, up + 1):
        late += [s] if s > 1 else []
        late += [planes - s] if s < planes - s else []
    steps = [("hop", 1), ("first", 0), ("second", 0), ("hop", planes - 1), ("order",), ("pass",)]
    steps += [("both", 0), ("second", 1), ("hop", 2)]
    for i, s in enumerate(late):
        steps += [("first", s)]
        if i > 0:
            steps += [("both", late[i - 1])]
        if 1 < s < up or s > up + 1:
            steps += [("hop", s + 1 if s < up else s - 1)]
        if i == 1:
            steps += [("relay", "both")]
        steps += [("second", s)]
        if i == 0:
            steps += [("mask",), ("relay", "first")]
        else:
            steps += [("absorb", late[i - 2] if i > 1 else 0, four)]
    last = late[-1]
    steps += [("both", last), ("absorb", 1, four[:1] + four[2:3])]
    steps += [("absorb", s, four) for s in late[-2:-1]]
    return steps + [("absorb", last, four[:3]), ("absorb", 1, four[1:2] + four[3:]), ("absorb", last, four[3:])]


def local(groups, n, edge, double_layer, projector, charge_in, charge_out, allowed, owner_slot_tile):
    planes = n // 4
    up = planes // 2
    got = {("own", 0): edge}
    total = None
    steps = plan(planes)

    def plane_shift(value, by):
        return lax.ppermute(value, "col", [(c, (c // 4 + by) % planes * 4 + c % 4) for c in range(n)])

    def across(value, which):
        flip = lambda r: which if r % 2 == 0 else 3 - which
        pairs = [(r * n + c, r * n + (c ^ flip(r))) for r in range(groups) for c in range(n)]
        return lax.ppermute(value, ("row", "col"), pairs)

    def row_shift(value, by):
        return lax.ppermute(value, "row", [(r, (r + by) % groups) for r in range(groups)])

    for step in steps:
        kind, s = step[0], step[-1 if len(step) < 3 else 1]
        if kind == "hop":
            before = s - 1 if s <= up else (s + 1) % planes
            got[("own", s)] = plane_shift(got[("own", before)], 1 if s <= up else -1)
        elif kind == "first":
            got[(kind, s)] = across(got[("own", s)], 1)
        elif kind == "second":
            got[(kind, s)] = across(got[("own", s)], 2)
        elif kind == "both":
            got[(kind, s)] = across(got[("first", s)], 2)
        elif kind == "relay":
            got[(s, 1)] = plane_shift(got[(s, 0)], 1)
        elif kind == "mask":
            masked = mask((charge_in, charge_out, allowed), double_layer)
        elif kind == "order":
            theirs = list(order(groups, owner_slot_tile, projector))
        elif kind == "pass":
            for k in range(1, groups):
                theirs[k] = row_shift(theirs[k], k)
        elif kind == "absorb":
            names = [(s, which) for which in step[2]]
            blocks = [got[(which, s)] for s, which in names]
            total = absorb(planes, names, masked, blocks, total, step == steps[-1])

    held = {}
    for k in range(1, groups):
        held[k] = row_shift(total, k)
    corner, contracted = own_corner(theirs[0], total)
    for k in range(1, groups - 1):
        corner = more_corner(theirs[k], held[k], corner)
    corner = corner_sum(theirs[groups - 1], held[groups - 1], corner)
    return contracted, corner


def solution(mesh):
    groups, n = mesh.shape["row"], mesh.shape["col"]

    def body(*arrays):
        return local(groups, n, *arrays)

    return jax.shard_map(
        body,
        mesh=mesh,
        in_specs=(P("row", "col"), P(None, "col"), P("row", None), P(), P("col"), P(), P()),
        out_specs=(P("row", "col"), P("row", "col")),
        check_vma=False,
    )
```

```python
import functools

import jax
import jax.numpy as jnp
from jax import lax
from jax.experimental import pallas as pl
from jax.experimental.pallas import tpu as pltpu
from jax.sharding import PartitionSpec as P


TILE = 128
PIECES = 2

VMEM = pl.BlockSpec(memory_space=pltpu.VMEM)
SMEM = pl.BlockSpec(memory_space=pltpu.SMEM)
FAR = pl.BlockSpec(memory_space=pl.ANY)


def near(*arrays):
    return [pltpu.with_memory_space_constraint(a, pltpu.VMEM) for a in arrays]


def far(*arrays):
    return [pltpu.with_memory_space_constraint(a, pltpu.HBM) for a in arrays]


def grant(mebibytes):
    return pltpu.CompilerParams(vmem_limit_bytes=mebibytes << 20)


def prepare_body(groups, chunks, cin, cout, allowed, slots, layer, projector, masked, *refs):
    outs, (held, met, layer_sems, sems) = refs[:groups], refs[groups:]
    rows, columns = layer.shape
    tiles = columns // TILE
    step = projector.shape[0] // chunks
    share = slots.shape[0] // groups
    row = lax.axis_index("row")

    def part(i):
        at = pl.ds(i * step, step)
        return pltpu.make_async_copy(projector.at[at, :], held.at[at, :], sems.at[i])

    def fetch(k):
        at = pl.ds(k * TILE, TILE)
        return pltpu.make_async_copy(layer.at[at, :], masked.at[at, :], layer_sems.at[k])

    for i in range(chunks):
        part(i).start()
    for q in range(allowed.shape[0]):
        bits = jnp.int32(0)
        for c in range(tiles):
            bits = bits + jnp.where(allowed[q, cout[c]] != 0, 1 << c, 0)
        met[q] = bits
    for k in range(rows // TILE):
        pl.when(met[cin[k]] != 0)(lambda k=k: fetch(k).start())
    for i in range(chunks):
        part(i).wait()
        for k in range(groups):
            for t in range(share):
                tile = slots[lax.rem(row + k, groups) * share + t]
                at = pl.ds(pl.multiple_of(tile * TILE, TILE), TILE)
                outs[k][t * TILE:(t + 1) * TILE, i * step:(i + 1) * step] = held[i * step:(i + 1) * step, at].T
    for k in range(rows // TILE):
        bits = met[cin[k]]

        @pl.when(bits == 0)
        def _():
            masked[k * TILE:(k + 1) * TILE, :] = jnp.zeros((TILE, columns), masked.dtype)

        @pl.when(bits != 0)
        def _():
            fetch(k).wait()
            for c in range(tiles):

                @pl.when(lax.bitwise_and(bits, 1 << c) == 0)
                def _():
                    masked[k * TILE:(k + 1) * TILE, c * TILE:(c + 1) * TILE] = jnp.zeros((TILE, TILE), masked.dtype)


def prepare(groups, tables, slots, layer, projector):
    chunks = 4
    rows, share = projector.shape[0], slots.shape[0] // groups
    masked, *ordered = pl.pallas_call(
        functools.partial(prepare_body, groups, chunks),
        out_shape=[pltpu.VMEM(layer.shape, layer.dtype)]
        + [pltpu.VMEM((share * TILE, rows), projector.dtype)] * groups,
        in_specs=[SMEM] * 4 + [FAR] * 2,
        out_specs=[VMEM] * (1 + groups),
        scratch_shapes=[
            pltpu.VMEM(projector.shape, projector.dtype),
            pltpu.SMEM((tables[2].shape[0],), jnp.int32),
            pltpu.SemaphoreType.DMA((layer.shape[0] // TILE,)),
            pltpu.SemaphoreType.DMA((chunks,)),
        ],
        compiler_params=grant(8),
        cost_estimate=pl.CostEstimate(flops=0, bytes_accessed=2 * layer.size + 4 * projector.size, transcendentals=0),
        name="prepare",
    )(*far(*tables, slots, layer, projector))
    return masked, ordered


def absorb_body(planes, names, fresh, at, masked, *refs):
    count = len(names)
    edges, out = refs[:count], refs[-1]
    depth = edges[0].shape[1]
    row, col = lax.axis_index("row"), lax.axis_index("col")
    plane, spot = lax.div(col, 4), lax.rem(col, 4)
    first = 1 + lax.rem(row, 2)
    flips = {"own": 0, "first": first, "second": 3 - first, "both": 3}
    layers = []
    for slot, which in names:
        block = lax.rem(plane + (planes - slot), planes) * 4 + (spot ^ flips[which])
        layers.append(masked[pl.ds(pl.multiple_of(block * depth, depth), depth), :])
    wide = jnp.concatenate([e[...] for e in edges], axis=1)
    total = jnp.dot(wide, jnp.concatenate(layers, axis=0), preferred_element_type=jnp.float32)
    if not fresh:
        total = total + refs[count][at:at + wide.shape[0], :]
    out[...] = total.astype(out.dtype)


def absorb(planes, names, masked, blocks, total, at=0, last=False):
    count, (rows, depth), columns = len(blocks), blocks[0].shape, masked.shape[1]
    extra = () if total is None else (total,)
    return pl.pallas_call(
        functools.partial(absorb_body, planes, names, total is None, at),
        out_shape=pltpu.VMEM((rows, columns), jnp.bfloat16 if last else jnp.float32),
        in_specs=[VMEM] * (1 + count + len(extra)),
        out_specs=VMEM,
        compiler_params=grant(8),
        cost_estimate=pl.CostEstimate(
            flops=2 * count * rows * depth * columns, bytes_accessed=4 * count * depth * columns, transcendentals=0
        ),
        name="absorb",
    )(*near(masked, *blocks, *extra))


def corner_term_body(start, fresh, writes, ordered, contracted, *refs):
    depth, sems = contracted.shape[0], refs[-1]
    refs, copies = list(refs), []
    total = None if fresh else refs.pop(0)
    pieces = [refs.pop(0) for _ in range(writes)]
    for i, piece in enumerate(pieces):
        at = pl.ds(i * piece.shape[0], piece.shape[0])
        copies.append(pltpu.make_async_copy(piece, refs[1].at[at, :], sems.at[i]))
        copies[-1].start()
    term = jnp.dot(ordered[:, start:start + depth], contracted[...], preferred_element_type=jnp.float32)
    refs[0][...] = term if fresh else total[...] + term
    for copy in copies:
        copy.wait()


def corner_term(start, ordered, contracted, total=None, pieces=()):
    (depth, columns), count = contracted.shape, len(pieces)
    shapes, specs = [pltpu.VMEM((ordered.shape[0], columns), jnp.float32)], [VMEM]
    if pieces:
        shapes += [jax.ShapeDtypeStruct((count * depth, columns), contracted.dtype)]
        specs += [FAR]
    more = (() if total is None else (total,)) + tuple(pieces)
    return pl.pallas_call(
        functools.partial(corner_term_body, start, total is None, count),
        out_shape=shapes,
        in_specs=[VMEM] * (2 + len(more)),
        out_specs=specs,
        scratch_shapes=[pltpu.SemaphoreType.DMA((max(count, 1),))],
        compiler_params=grant(8),
        cost_estimate=pl.CostEstimate(
            flops=2 * ordered.shape[0] * contracted.size, bytes_accessed=2 * contracted.size, transcendentals=0
        ),
        name="corner_term",
    )(*near(ordered, contracted, *more))


def corner_body(start, chunks, ordered, contracted, total, out, held, sems):
    step, depth = ordered.shape[0] // chunks, contracted.shape[0]
    copies = []
    for i in range(chunks):
        at = pl.ds(i * step, step)
        term = jnp.dot(ordered[at, start:start + depth], contracted[...], preferred_element_type=jnp.float32)
        held[at, :] = (total[at, :] + term).astype(held.dtype)
        copies.append(pltpu.make_async_copy(held.at[at, :], out.at[at, :], sems.at[i]))
        copies[-1].start()
    for copy in copies:
        copy.wait()


def corner_sum(start, ordered, contracted, total):
    chunks, kind = 8, jnp.bfloat16
    rows, columns = total.shape
    return pl.pallas_call(
        functools.partial(corner_body, start, chunks),
        out_shape=jax.ShapeDtypeStruct((rows, columns), kind),
        in_specs=[VMEM] * 3,
        out_specs=FAR,
        scratch_shapes=[pltpu.VMEM((rows, columns), kind), pltpu.SemaphoreType.DMA((chunks,))],
        compiler_params=grant(8),
        cost_estimate=pl.CostEstimate(
            flops=2 * ordered.shape[0] * contracted.size, bytes_accessed=2 * rows * columns, transcendentals=0
        ),
        name="corner",
    )(*near(ordered, contracted, total))


def plan(planes):
    up = planes // 2
    whole = lambda s: tuple((s, kind) for kind in ("own", "first", "second", "both"))
    late = []
    for s in range(1, up + 1):
        late += [s] if s > 1 else []
        late += [planes - s] if s < planes - s else []
    steps = [("hop", 1), ("first", 0), ("second", 0), ("hop", planes - 1), ("prepare",)]
    steps += [("both", 0), ("hop", 2), ("second", 1)]
    for i, s in enumerate(late):
        steps += [("first", s)]
        hop = [("hop", s + 1 if s < up else s - 1)] if 1 < s < up or s > up + 1 else []
        if i == 0:
            steps += hop + [("pass",), ("relay", "first"), ("second", s)]
            continue
        if i == 1:
            steps += [("absorb", 0, whole(0) + ((1, "own"), (1, "second")))]
        else:
            steps += [("absorb", late[i - 2], whole(late[i - 2]))]
        steps += [("both", late[i - 1]), ("second", s)] + hop
        if i == 1:
            steps += [("relay", "both")]
    last = late[-1]
    steps += [("both", last)] + [("absorb", s, whole(s)) for s in late[-2:-1]]
    return steps + [("absorb", last, ((last, "own"), (last, "second"), (1, "first"), (1, "both")))]


def last_slot(planes):
    return next(step[1] for step in reversed(plan(planes)) if step[0] == "both")


def local(groups, n, edge, double_layer, projector, charge_in, charge_out, allowed, owner_slot_tile):
    planes = n // 4
    up = planes // 2
    last, height = last_slot(planes), edge.shape[0] // PIECES
    got = {("own", 0): edge}
    total = None
    steps = plan(planes)

    def plane_shift(value, by):
        return lax.ppermute(value, "col", [(c, (c // 4 + by) % planes * 4 + c % 4) for c in range(n)])

    def across(value, which):
        flip = lambda r: which if r % 2 == 0 else 3 - which
        pairs = [(r * n + c, r * n + (c ^ flip(r))) for r in range(groups) for c in range(n)]
        return lax.ppermute(value, ("row", "col"), pairs)

    def row_shift(value, by):
        return lax.ppermute(value, "row", [(r, (r + by) % groups) for r in range(groups)])

    for step in steps:
        kind, s = step[0], step[-1 if len(step) < 3 else 1]
        if kind == "hop":
            before = s - 1 if s <= up else (s + 1) % planes
            got[("own", s)] = plane_shift(got[("own", before)], 1 if s <= up else -1)
        elif s == last and kind in ("first", "both"):
            for i in range(PIECES):
                if kind == "first":
                    piece = across(got[("own", s)][i * height:(i + 1) * height], 1)
                else:
                    piece = across(got[("firsts", i)], 2)
                got[(kind + "s", i)] = piece
        elif kind == "first":
            got[(kind, s)] = across(got[("own", s)], 1)
        elif kind == "second":
            got[(kind, s)] = across(got[("own", s)], 2)
        elif kind == "both":
            got[(kind, s)] = across(got[("first", s)], 2)
        elif kind == "relay":
            got[(s, 1)] = plane_shift(got[(s, 0)], 1)
        elif kind == "prepare":
            tables = (charge_in, charge_out, allowed)
            masked, theirs = prepare(groups, tables, owner_slot_tile, double_layer, projector)
        elif kind == "pass":
            for k in range(1, groups):
                theirs[k] = row_shift(theirs[k], k)
        elif kind == "absorb":
            names = step[2]
            blocks = [got[(which, slot)] for slot, which in names]
            total = absorb(planes, names, masked, blocks, total)

    names = [(last, "first"), (last, "both")]
    pieces, held, corner = [], [], None
    for i in range(PIECES):
        blocks = [got[("firsts", i)], got[("boths", i)]]
        pieces.append(absorb(planes, names, masked, blocks, total, i * height, True))
        for k in range(1, groups):
            held.append((k, i * height, row_shift(pieces[i], k)))
        out = corner_term(i * height, theirs[0], pieces[i], corner, pieces if i == PIECES - 1 else ())
        corner = out[0]
    contracted = out[1]
    for k, start, piece in held[:-1]:
        corner = corner_term(start, theirs[k], piece, corner)[0]
    k, start, piece = held[-1]
    corner = corner_sum(start, theirs[k], piece, corner)
    return contracted, corner


def solution(mesh):
    groups, n = mesh.shape["row"], mesh.shape["col"]

    def body(*arrays):
        return local(groups, n, *arrays)

    return jax.shard_map(
        body,
        mesh=mesh,
        in_specs=(P("row", "col"), P(None, "col"), P("row", None), P(), P("col"), P(), P()),
        out_specs=(P("row", "col"), P("row", "col")),
        check_vma=False,
    )
```

```python
import functools

import jax
import jax.numpy as jnp
from jax import lax
from jax.experimental import pallas as pl
from jax.experimental.pallas import tpu as pltpu
from jax.sharding import PartitionSpec as P


TILE = 128
PIECES = 2

VMEM = pl.BlockSpec(memory_space=pltpu.VMEM)
SMEM = pl.BlockSpec(memory_space=pltpu.SMEM)
FAR = pl.BlockSpec(memory_space=pl.ANY)


def near(*arrays):
    return [pltpu.with_memory_space_constraint(a, pltpu.VMEM) for a in arrays]


def far(*arrays):
    return [pltpu.with_memory_space_constraint(a, pltpu.HBM) for a in arrays]


def grant(mebibytes):
    return pltpu.CompilerParams(vmem_limit_bytes=mebibytes << 20)


def prepare_body(groups, chunks, cin, cout, allowed, slots, layer, projector, masked, *refs):
    outs, (held, met, layer_sems, sems) = refs[:groups], refs[groups:]
    rows, columns = layer.shape
    tiles = columns // TILE
    step = projector.shape[0] // chunks
    share = slots.shape[0] // groups
    row = lax.axis_index("row")

    def part(i):
        at = pl.ds(i * step, step)
        return pltpu.make_async_copy(projector.at[at, :], held.at[at, :], sems.at[i])

    def fetch(k):
        at = pl.ds(k * TILE, TILE)
        return pltpu.make_async_copy(layer.at[at, :], masked.at[at, :], layer_sems.at[k])

    for i in range(chunks):
        part(i).start()
    for q in range(allowed.shape[0]):
        bits = jnp.int32(0)
        for c in range(tiles):
            bits = bits + jnp.where(allowed[q, cout[c]] != 0, 1 << c, 0)
        met[q] = bits
    for k in range(rows // TILE):
        pl.when(met[cin[k]] != 0)(lambda k=k: fetch(k).start())
    for i in range(chunks):
        part(i).wait()
        for k in range(groups):
            for t in range(share):
                tile = slots[lax.rem(row + k, groups) * share + t]
                at = pl.ds(pl.multiple_of(tile * TILE, TILE), TILE)
                outs[k][t * TILE:(t + 1) * TILE, i * step:(i + 1) * step] = held[i * step:(i + 1) * step, at].T
    for k in range(rows // TILE):
        bits = met[cin[k]]

        @pl.when(bits == 0)
        def _():
            masked[k * TILE:(k + 1) * TILE, :] = jnp.zeros((TILE, columns), masked.dtype)

        @pl.when(bits != 0)
        def _():
            fetch(k).wait()
            for c in range(tiles):

                @pl.when(lax.bitwise_and(bits, 1 << c) == 0)
                def _():
                    masked[k * TILE:(k + 1) * TILE, c * TILE:(c + 1) * TILE] = jnp.zeros((TILE, TILE), masked.dtype)


def prepare(groups, tables, slots, layer, projector):
    chunks = 4
    rows, share = projector.shape[0], slots.shape[0] // groups
    masked, *ordered = pl.pallas_call(
        functools.partial(prepare_body, groups, chunks),
        out_shape=[pltpu.VMEM(layer.shape, layer.dtype)]
        + [pltpu.VMEM((share * TILE, rows), projector.dtype)] * groups,
        in_specs=[SMEM] * 4 + [FAR] * 2,
        out_specs=[VMEM] * (1 + groups),
        scratch_shapes=[
            pltpu.VMEM(projector.shape, projector.dtype),
            pltpu.SMEM((tables[2].shape[0],), jnp.int32),
            pltpu.SemaphoreType.DMA((layer.shape[0] // TILE,)),
            pltpu.SemaphoreType.DMA((chunks,)),
        ],
        compiler_params=grant(8),
        cost_estimate=pl.CostEstimate(flops=0, bytes_accessed=2 * layer.size + 4 * projector.size, transcendentals=0),
        name="prepare",
    )(*far(*tables, slots, layer, projector))
    return masked, ordered


def absorb_body(planes, names, fresh, at, masked, *refs):
    count = len(names)
    edges, out = refs[:count], refs[-1]
    depth = edges[0].shape[1]
    row, col = lax.axis_index("row"), lax.axis_index("col")
    plane, spot = lax.div(col, 4), lax.rem(col, 4)
    first = 1 + lax.rem(row, 2)
    flips = {"own": 0, "first": first, "second": 3 - first, "both": 3}
    layers = []
    for slot, which in names:
        block = lax.rem(plane + (planes - slot), planes) * 4 + (spot ^ flips[which])
        layers.append(masked[pl.ds(pl.multiple_of(block * depth, depth), depth), :])
    rows = out.shape[0]
    wide = jnp.concatenate([e[...] if e.shape[0] == rows else e[at:at + rows, :] for e in edges], axis=1)
    total = jnp.dot(wide, jnp.concatenate(layers, axis=0), preferred_element_type=jnp.float32)
    if not fresh:
        total = total + refs[count][at:at + rows, :]
    out[...] = total.astype(out.dtype)


def absorb(planes, names, masked, blocks, total, at=0, last=False):
    count, (rows, depth), columns = len(blocks), blocks[0].shape, masked.shape[1]
    extra = () if total is None else (total,)
    return pl.pallas_call(
        functools.partial(absorb_body, planes, names, total is None, at),
        out_shape=pltpu.VMEM((rows, columns), jnp.bfloat16 if last else jnp.float32),
        in_specs=[VMEM] * (1 + count + len(extra)),
        out_specs=VMEM,
        compiler_params=grant(8),
        cost_estimate=pl.CostEstimate(
            flops=2 * count * rows * depth * columns, bytes_accessed=4 * count * depth * columns, transcendentals=0
        ),
        name="absorb",
    )(*near(masked, *blocks, *extra))


def corner_term_body(start, fresh, writes, ordered, contracted, *refs):
    depth, sems = contracted.shape[0], refs[-1]
    refs, copies = list(refs), []
    total = None if fresh else refs.pop(0)
    pieces = [refs.pop(0) for _ in range(writes)]
    for i, piece in enumerate(pieces):
        at = pl.ds(i * piece.shape[0], piece.shape[0])
        copies.append(pltpu.make_async_copy(piece, refs[1].at[at, :], sems.at[i]))
        copies[-1].start()
    term = jnp.dot(ordered[:, start:start + depth], contracted[...], preferred_element_type=jnp.float32)
    refs[0][...] = term if fresh else total[...] + term
    for copy in copies:
        copy.wait()


def corner_term(start, ordered, contracted, total=None, pieces=()):
    (depth, columns), count = contracted.shape, len(pieces)
    shapes, specs = [pltpu.VMEM((ordered.shape[0], columns), jnp.float32)], [VMEM]
    if pieces:
        shapes += [jax.ShapeDtypeStruct((count * depth, columns), contracted.dtype)]
        specs += [FAR]
    more = (() if total is None else (total,)) + tuple(pieces)
    return pl.pallas_call(
        functools.partial(corner_term_body, start, total is None, count),
        out_shape=shapes,
        in_specs=[VMEM] * (2 + len(more)),
        out_specs=specs,
        scratch_shapes=[pltpu.SemaphoreType.DMA((max(count, 1),))],
        compiler_params=grant(8),
        cost_estimate=pl.CostEstimate(
            flops=2 * ordered.shape[0] * contracted.size, bytes_accessed=2 * contracted.size, transcendentals=0
        ),
        name="corner_term",
    )(*near(ordered, contracted, *more))


def corner_body(start, chunks, ordered, contracted, total, out, held, sems):
    step, depth = ordered.shape[0] // chunks, contracted.shape[0]
    copies = []
    for i in range(chunks):
        at = pl.ds(i * step, step)
        term = jnp.dot(ordered[at, start:start + depth], contracted[...], preferred_element_type=jnp.float32)
        held[at, :] = (total[at, :] + term).astype(held.dtype)
        copies.append(pltpu.make_async_copy(held.at[at, :], out.at[at, :], sems.at[i]))
        copies[-1].start()
    for copy in copies:
        copy.wait()


def corner_sum(start, ordered, contracted, total):
    chunks, kind = 8, jnp.bfloat16
    rows, columns = total.shape
    return pl.pallas_call(
        functools.partial(corner_body, start, chunks),
        out_shape=jax.ShapeDtypeStruct((rows, columns), kind),
        in_specs=[VMEM] * 3,
        out_specs=FAR,
        scratch_shapes=[pltpu.VMEM((rows, columns), kind), pltpu.SemaphoreType.DMA((chunks,))],
        compiler_params=grant(8),
        cost_estimate=pl.CostEstimate(
            flops=2 * ordered.shape[0] * contracted.size, bytes_accessed=2 * rows * columns, transcendentals=0
        ),
        name="corner",
    )(*near(ordered, contracted, total))


def plan(planes):
    up, below = planes // 2, planes - 1
    whole = lambda s: tuple((s, kind) for kind in ("own", "first", "second", "both"))
    hop = lambda s: [("hop", s + 1)] if s < up else [("hop", s - 1)] if s > up + 1 else []
    late = []
    for s in range(2, up + 1):
        late += [s] + ([planes - s] if s < planes - s else [])
    steps = [("hop", 1), ("first", 0), ("second", 0), ("hop", below), ("prepare",)]
    steps += [("both", 0), ("hop", 2), ("first", 1), ("second", 1), ("pass",)]
    steps += hop(below) + [("second", below), ("relay", "first")]
    for before, s in zip([1] + late, late):
        steps += [("first", s), ("both", before)] + hop(s)
        steps += [("second", s)]
        if before == 1:
            steps += [("relay", "both")]
    last = late[-1]
    steps += [("both", last), ("absorb", 0, whole(0) + whole(1))]
    steps += [("absorb", s, whole(s)) for s in late[:-1]]
    rest = ((last, "own"), (last, "second"), (below, "own"), (below, "first"), (below, "second"))
    return steps + [("absorb", last, rest)]


def last_slot(planes):
    return next(step[1] for step in reversed(plan(planes)) if step[0] == "both")


def local(groups, n, edge, double_layer, projector, charge_in, charge_out, allowed, owner_slot_tile):
    planes = n // 4
    up = planes // 2
    last, height = last_slot(planes), edge.shape[0] // PIECES
    got = {("own", 0): edge}
    total = None
    steps = plan(planes)

    def plane_shift(value, by):
        return lax.ppermute(value, "col", [(c, (c // 4 + by) % planes * 4 + c % 4) for c in range(n)])

    def across(value, which):
        flip = lambda r: which if r % 2 == 0 else 3 - which
        pairs = [(r * n + c, r * n + (c ^ flip(r))) for r in range(groups) for c in range(n)]
        return lax.ppermute(value, ("row", "col"), pairs)

    def row_shift(value, by):
        return lax.ppermute(value, "row", [(r, (r + by) % groups) for r in range(groups)])

    for step in steps:
        kind, s = step[0], step[-1 if len(step) < 3 else 1]
        if kind == "hop":
            before = s - 1 if s <= up else (s + 1) % planes
            got[("own", s)] = plane_shift(got[("own", before)], 1 if s <= up else -1)
        elif s == last and kind in ("first", "both"):
            for i in range(PIECES):
                if kind == "first":
                    piece = across(got[("own", s)][i * height:(i + 1) * height], 1)
                else:
                    piece = across(got[("firsts", i)], 2)
                got[(kind + "s", i)] = piece
        elif kind == "first":
            got[(kind, s)] = across(got[("own", s)], 1)
        elif kind == "second":
            got[(kind, s)] = across(got[("own", s)], 2)
        elif kind == "both":
            got[(kind, s)] = across(got[("first", s)], 2)
        elif kind == "relay":
            got[(s, planes - 1)] = plane_shift(got[(s, 0)], -1)
        elif kind == "prepare":
            tables = (charge_in, charge_out, allowed)
            masked, theirs = prepare(groups, tables, owner_slot_tile, double_layer, projector)
        elif kind == "pass":
            for k in range(1, groups):
                theirs[k] = row_shift(theirs[k], k)
        elif kind == "absorb":
            names = step[2]
            blocks = [got[(which, slot)] for slot, which in names]
            total = absorb(planes, names, masked, blocks, total)

    names = [(last, "first"), (last, "both"), (planes - 1, "both")]
    pieces, held, corner = [], [], None
    for i in range(PIECES):
        blocks = [got[("firsts", i)], got[("boths", i)], got[("both", planes - 1)]]
        pieces.append(absorb(planes, names, masked, blocks, total, i * height, True))
        for k in range(1, groups):
            held.append((k, i * height, row_shift(pieces[i], k)))
        out = corner_term(i * height, theirs[0], pieces[i], corner, pieces if i == PIECES - 1 else ())
        corner = out[0]
    contracted = out[1]
    for k, start, piece in held[:-1]:
        corner = corner_term(start, theirs[k], piece, corner)[0]
    k, start, piece = held[-1]
    corner = corner_sum(start, theirs[k], piece, corner)
    return contracted, corner


def solution(mesh):
    groups, n = mesh.shape["row"], mesh.shape["col"]

    def body(*arrays):
        return local(groups, n, *arrays)

    return jax.shard_map(
        body,
        mesh=mesh,
        in_specs=(P("row", "col"), P(None, "col"), P("row", None), P(), P("col"), P(), P()),
        out_specs=(P("row", "col"), P("row", "col")),
        check_vma=False,
    )
```
